32 devices in a mesh: blk: 8 (over y, x, core), batch: 4 (over z).
Axes of the slice: x: 2, y: 2, z: 4, core: 2. Of those that a mesh axis runs over, the one named last changes fastest.
Arguments:
- query_base: bfloat16 [32, 36864], P(('batch', 'blk')), may hold values from -14 to 14
- query_latent: bfloat16 [32, 1536], P(('batch', 'blk')), may hold values from -6 to 6
- tenant_ids: int32 [32], P('batch'), may hold values from 0 to 3
- adapter_qa: bfloat16 [4, 1536, 16], replicated, may hold values from -0.15625 to 0.15625
- adapter_qb: bfloat16 [4, 16, 36864], replicated, may hold values from -0.29882812 to 0.29882812
- prefix_cache: bfloat16 [32768, 576], P('blk'), may hold values from -6 to 6
- prefix_mask: int32 [32, 256], P('batch', 'blk'), may hold values 0 or 1
- suffix_cache: bfloat16 [32, 4096, 576], P(('batch', 'blk')), may hold values from -6 to 6
- suffix_blocks: int32 [8, 4], P('blk'), may hold values from 1 to 32, 40 in all within a row
- new_latent: bfloat16 [32, 576], P(('batch', 'blk')), may hold values from -6 to 6
- value_up: bfloat16 [64, 512, 128], P('blk'), may hold values from -0.25 to 0.25
- out_weight: bfloat16 [8192, 7168], P('blk'), may hold values from -0.0625 to 0.0625
- adapter_oa: bfloat16 [4, 8192, 16], P(None, 'blk'), may hold values from -0.0625 to 0.0625
- adapter_ob: bfloat16 [4, 16, 7168], replicated, may hold values from -1.5 to 1.5
Outputs:
- attention_out: bfloat16 [32, 7168], P(('batch', 'blk'))
The draws below stay inside these ranges and needn't reach their ends.
Inputs may be any that keep to these rules, and one draw needn't show every extreme that they name: `suffix_blocks`: each row holds 40 blocks in all, and its largest entry is exactly 32.
All inputs are finite; a program needn't handle non-finite values. No bound on the sum of `prefix_mask` on one device may be relied on, other than what follows from the above.
Results may differ from the reference program's by a relative error of at most 0.025.
Values may be sent and summed in bfloat16 or wider, within the bound.
A program may use at most 128 MiB of HBM per device.

```python
import math
import jax
import jax.numpy as jnp
import numpy as np
from jax import lax

D = 7168
QL = 1536
H = 64
LAT = 512
VH = 128
QK = 192
RANK = 16
TEN = 4
BLOCK = 128
REQ_DEV = 1
SB_AVG = 10
SB_MAX = 32
KV = 576
PBLK = 256
PTOK = 32768
REQ = 32
COLUMN = 4
SUF = 4096
N_BLK = 8
N_BATCH = 4


def draw_prefix_cache(key, part):
    own_key = jax.random.fold_in(key, 11)
    values = jnp.clip(jax.random.normal(own_key, (PTOK, KV), jnp.float32), -6.0, 6.0)
    return values.astype(jnp.bfloat16)


def draw_query_base(key, part):
    own_key = jax.random.fold_in(key, 13)
    values = jnp.clip(0.5 * jax.random.normal(own_key, (REQ, H, KV), jnp.float32), -3.0, 3.0)
    return values.reshape(REQ, H * KV).astype(jnp.bfloat16)


def touch_ends(array, key, smallest, largest):
    place = [jax.random.randint(jax.random.fold_in(key, axis), (), 0, length) for axis, length in enumerate(array.shape)]
    widest = array.shape.index(max(array.shape))
    next_to = place[:widest] + [(place[widest] + 1) % array.shape[widest]] + place[widest + 1:]
    return array.at[tuple(place)].set(smallest).at[tuple(next_to)].set(largest)


def block_scale(rng, extent, split, least, high):
    def one(position, blocks):
        steps = jax.random.uniform(jax.random.fold_in(jax.random.fold_in(rng, 6), position), (blocks,), jnp.float32, least / len(split), high / len(split))
        return jnp.repeat(jnp.exp(steps), extent[position] // blocks).reshape((-1,) + (1,) * (len(extent) - position - 1))

    gain = one(*split[0])
    for cut in split[1:]:
        gain = gain * one(*cut)
    return gain


def length_profile(count, total, reach, skew):
    loads = [(1 << 20) // math.isqrt(rank ** skew) + 1 for rank in range(2, count + 1)]
    surplus, counts = total - reach - (count - 1), [1] * (count - 1)
    while surplus > 0:
        candidates = [i for i in range(count - 1) if counts[i] < reach]
        whole, budget = sum([loads[i] for i in candidates]), surplus
        for i in candidates:
            more = min(reach - counts[i], max(1, budget * loads[i] // whole), surplus)
            counts[i] = counts[i] + more
            surplus = surplus - more
    return np.array([reach] + counts)


def uneven_parts(key, number_of, total, reach, skew):
    if number_of == 2:
        one = jax.random.randint(key, (), max(1, total - reach), min(reach, total - 1) + 1)
        return jnp.stack([one, total - one])
    sizes = jnp.asarray(length_profile(number_of, total, reach, skew), jnp.int32)
    couples = (number_of - 1) // 2
    donor, receiver = sizes[1:1 + 2 * couples:2], sizes[2:2 + 2 * couples:2]
    room = jnp.minimum(donor - 1, reach - receiver)
    moved = jax.random.randint(jax.random.fold_in(key, 1), (couples,), 0, 1 << 20) % (room + 1)
    sizes = sizes.at[1:1 + 2 * couples:2].set(donor - moved).at[2:2 + 2 * couples:2].set(receiver + moved)
    return sizes[jax.random.permutation(jax.random.fold_in(key, 2), number_of)]


def gaussian(rng, shape, width, bound, pieces=(), kind=jnp.bfloat16):
    level = block_scale(rng, shape, pieces, -0.22, 0.18) if pieces else 1.0
    entries = jax.random.normal(rng, shape, jnp.float32) * width * level
    return jnp.minimum(jnp.maximum(entries, -bound), bound).astype(kind)


def setup_inputs(seed: int = 0) -> dict:
    streams_of = jax.random.split(jax.random.key(seed), 15)
    query_base = draw_query_base(jax.random.fold_in(streams_of[14], 71), 0)
    query_latent = gaussian(streams_of[1], (REQ, QL), 1.0, 6.0, ((0, 32),))
    tenant_ids = touch_ends(jax.random.randint(streams_of[2], (REQ,), 0, TEN), jax.random.fold_in(streams_of[2], 1), 0, TEN - 1).astype(jnp.int32)
    adapter_qa = gaussian(streams_of[3], (TEN, QL, RANK), QL ** -0.5, 0.15625)
    adapter_qb = gaussian(streams_of[4], (TEN, RANK, H * KV), 0.05, 0.29882812)
    prefix_cache = draw_prefix_cache(jax.random.fold_in(streams_of[14], 71), 0)
    prefix_mask = touch_ends((jax.random.randint(streams_of[6], (REQ, PBLK), 0, 6) < 1).astype(jnp.int32), jax.random.fold_in(streams_of[6], 1), 0, 1)
    suffix_cache = gaussian(streams_of[7], (REQ, SUF, KV), 1.0, 6.0, ((0, 32),))
    suffix_blocks = jax.vmap(lambda own: uneven_parts(own, COLUMN, COLUMN * SB_AVG, SB_MAX, 2))(jax.random.split(streams_of[8], N_BLK)).reshape((N_BLK, COLUMN)).astype(jnp.int32)
    new_latent = gaussian(streams_of[9], (REQ, KV), 1.0, 6.0, ((0, 32),))
    value_up = gaussian(streams_of[10], (H, LAT, VH), LAT ** -0.5, 0.25, ((0, 8),))
    out_weight = gaussian(streams_of[11], (H * VH, D), (H * VH) ** -0.5, 0.0625, ((0, 8),))
    adapter_oa = gaussian(streams_of[12], (TEN, H * VH, RANK), (H * VH) ** -0.5, 0.0625, ((1, 8),))
    adapter_ob = gaussian(streams_of[13], (TEN, RANK, D), 0.25, 1.5)
    return dict(query_base=query_base, query_latent=query_latent, tenant_ids=tenant_ids, adapter_qa=adapter_qa, adapter_qb=adapter_qb, prefix_cache=prefix_cache, prefix_mask=prefix_mask, suffix_cache=suffix_cache, suffix_blocks=suffix_blocks, new_latent=new_latent, value_up=value_up, out_weight=out_weight, adapter_oa=adapter_oa, adapter_ob=adapter_ob)


def request_lengths(suffix_blocks):
    layout = suffix_blocks.reshape(N_BLK, N_BATCH, REQ_DEV)
    return jnp.transpose(layout, (1, 0, 2)).reshape(REQ)


def reference(query_base, query_latent, tenant_ids, adapter_qa, adapter_qb, prefix_cache, prefix_mask, suffix_cache, suffix_blocks, new_latent, value_up, out_weight, adapter_oa, adapter_ob):
    score_scale = QK ** -0.5
    delta_query = jnp.zeros((REQ, H * KV), jnp.float32)
    for tenant in range(TEN):
        low_rank = jnp.dot(query_latent, adapter_qa[tenant], preferred_element_type=jnp.float32).astype(jnp.bfloat16)
        added = jnp.dot(low_rank, adapter_qb[tenant], preferred_element_type=jnp.float32)
        delta_query = jnp.where((tenant_ids == tenant)[:, None], added, delta_query)
    query = (query_base.astype(jnp.float32) + delta_query).astype(jnp.bfloat16).reshape(REQ, H, KV)
    lengths = request_lengths(suffix_blocks)
    prefix_values = prefix_cache[:, :LAT]
    contract = (((1,), (1,)), ((), ()))

    def attend(item):
        queries, mask_row, private, length, fresh = item
        token_live = jnp.repeat(mask_row > 0, BLOCK)
        pre_scores = lax.dot_general(queries, prefix_cache, contract, preferred_element_type=jnp.float32) * score_scale
        pre_scores = jnp.where(token_live[None, :], pre_scores, -jnp.inf)
        suf_scores = lax.dot_general(queries, private, contract, preferred_element_type=jnp.float32) * score_scale
        suf_live = jnp.arange(SUF, dtype=jnp.int32) < length * BLOCK
        suf_scores = jnp.where(suf_live[None, :], suf_scores, -jnp.inf)
        new_scores = jnp.dot(queries, fresh, preferred_element_type=jnp.float32) * score_scale
        peak = jnp.maximum(jnp.maximum(jnp.max(pre_scores, axis=1), jnp.max(suf_scores, axis=1)), new_scores)
        pre_weight = jnp.exp(pre_scores - peak[:, None])
        suf_weight = jnp.exp(suf_scores - peak[:, None])
        new_weight = jnp.exp(new_scores - peak)
        total = jnp.sum(pre_weight, axis=1) + jnp.sum(suf_weight, axis=1) + new_weight
        summed = jnp.dot(pre_weight.astype(jnp.bfloat16), prefix_values, preferred_element_type=jnp.float32)
        summed = summed + jnp.dot(suf_weight.astype(jnp.bfloat16), private[:, :LAT], preferred_element_type=jnp.float32)
        summed = summed + new_weight.astype(jnp.bfloat16).astype(jnp.float32)[:, None] * fresh[:LAT].astype(jnp.float32)[None, :]
        return (summed / total[:, None]).astype(jnp.bfloat16)

    context = lax.map(attend, (query, prefix_mask, suffix_cache, lengths, new_latent))
    head_out = jnp.einsum('rhl,hlv->rhv', context.astype(jnp.float32), value_up.astype(jnp.float32))
    head_out = head_out.astype(jnp.bfloat16).reshape(REQ, H * VH)
    projected = jnp.dot(head_out, out_weight, preferred_element_type=jnp.float32)
    delta_out = jnp.zeros((REQ, D), jnp.float32)
    for tenant in range(TEN):
        low_rank = jnp.dot(head_out, adapter_oa[tenant], preferred_element_type=jnp.float32)
        added = jnp.dot(low_rank, adapter_ob[tenant].astype(jnp.float32), precision=lax.Precision.HIGHEST)
        delta_out = jnp.where((tenant_ids == tenant)[:, None], added, delta_out)
    return (projected + delta_out).astype(jnp.bfloat16)
```

```python
import functools
import math

import jax
import jax.numpy as jnp
from jax import lax
from jax.experimental import pallas as pl
from jax.experimental.pallas import tpu as pltpu
from jax.sharding import PartitionSpec as P

D = 7168
H = 64
LAT = 512
QK = 192
RANK = 16
BLOCK = 128
KV = 576
FLOOR = -1e30
CHUNK = 1024
GROUP = 4
PARTS = 8
SCALE = QK ** (-0.5) * math.log2(math.e)
F32 = jnp.float32
BF16 = jnp.bfloat16
NT = (((1,), (1,)), ((), ()))


def split3(x):
    hi = x.astype(BF16).astype(F32)
    rest = x - hi
    mid = rest.astype(BF16).astype(F32)
    return hi, mid, rest - mid


def attend_chunk(state, queries, keys, bias):
    peak, total, sums = state
    scores = lax.dot_general(queries, keys, NT, preferred_element_type=F32) * SCALE + bias
    fresh = jnp.maximum(peak, jnp.max(scores, axis=1, keepdims=True))
    weights = jnp.exp2(scores - fresh)
    keep = jnp.exp2(peak - fresh)
    total = total * keep + jnp.sum(weights, axis=1, keepdims=True)
    sums = sums * keep + jnp.dot(weights.astype(BF16), keys[:, :LAT], preferred_element_type=F32)
    return fresh, total, sums


def kernel(
    n,
    tenant_ref, length_ref,
    base_ref, latent_ref, qa_hbm, qb_hbm, prefix_hbm, mask_ref, suffix_hbm, new_ref,
    up_hbm, weight_hbm, oa_hbm, ob_hbm,
    out_ref,
    qa, qb, prefix, suffix, up, weight, oa, ob,
    pair_scr, head_scr, queries, bias_scr, sums_scr, stat_scr, send, recv, ctx_scr, row_scr, out_send, out_recv,
    load_sem, q_send, q_recv, p_send, p_recv, o_send, o_recv,
):
    me = lax.axis_index("blk")
    bits = n.bit_length() - 1
    heads_here = H // n

    def peer(k):
        total = 0
        for b in range(bits):
            total = total + lax.rem(lax.div(me, 1 << b) + (k >> b & 1), 2) * (1 << b)
        return total

    peers = [peer(k) for k in range(n)]
    loads = [
        pltpu.make_async_copy(src, dst, load_sem.at[i])
        for i, (src, dst) in enumerate(
            [(qa_hbm, qa), (qb_hbm, qb), (suffix_hbm.at[0], suffix), (prefix_hbm, prefix),
             (up_hbm, up), (oa_hbm, oa), (ob_hbm, ob), (weight_hbm, weight)]
        )
    ]
    for load in loads:
        load.start()

    barrier = pltpu.get_barrier_semaphore()
    for k in range(1, n):
        pl.semaphore_signal(barrier, inc=1, device_id={"blk": peers[k]}, device_id_type=pl.DeviceIdType.MESH)

    loads[0].wait()
    own_tenant = tenant_ref[me]
    latent = jnp.broadcast_to(latent_ref[...].astype(F32), (16, latent_ref.shape[1])).astype(BF16)
    tenants = qa.shape[0]
    lows = []
    for t in range(tenants):
        low = jnp.dot(latent, qa[t], preferred_element_type=F32)
        lows.append(jnp.where(own_tenant == t, low, 0.0))
    low_spread = jnp.concatenate(lows, axis=1).astype(BF16)
    loads[1].wait()
    row_id = lax.broadcasted_iota(jnp.int32, (8, 2 * KV), 0)
    for i in range(H // 16):
        columns = slice(i * 16 * KV, (i + 1) * 16 * KV)
        up_map = qb[:, :, columns].reshape(tenants * RANK, 16 * KV)
        delta = jnp.dot(low_spread, up_map, preferred_element_type=F32)[:8]
        full = delta + base_ref[:, columns].astype(F32)
        rows = full[:, : 2 * KV]
        for p in range(1, 8):
            rows = jnp.where(row_id == p, full[:, p * 2 * KV : (p + 1) * 2 * KV], rows)
        pair_scr[i * 8 : (i + 1) * 8, :] = rows
    even = pair_scr[:, :KV]
    odd = pair_scr[:, KV:]
    tiles = [(lt, min(128, KV - lt * 128)) for lt in range(pl.cdiv(KV, 128))]
    for lt, width in tiles:
        head_scr[lt, pl.ds(0, H // 2, stride=2), :width] = even[:, lt * 128 : lt * 128 + width]
        head_scr[lt, pl.ds(1, H // 2, stride=2), :width] = odd[:, lt * 128 : lt * 128 + width]
    for lt, width in tiles:
        queries[0, :, lt * 128 : lt * 128 + width] = head_scr[lt, :, :width].astype(BF16)

    pl.semaphore_wait(barrier, n - 1)
    q_copies = []
    for k in range(1, n):
        copy = pltpu.make_async_remote_copy(
            src_ref=queries.at[0], dst_ref=queries.at[k], send_sem=q_send.at[k], recv_sem=q_recv.at[k],
            device_id={"blk": peers[k]}, device_id_type=pl.DeviceIdType.MESH)
        copy.start()
        q_copies.append(copy)

    live = jnp.where(mask_ref[...] > 0, 0.0, -jnp.inf).astype(F32)
    for b in range(mask_ref.shape[1]):
        bias_scr[:, b * BLOCK : (b + 1) * BLOCK] = jnp.broadcast_to(live[:, b : b + 1], (n, BLOCK))

    own = queries[0]
    fresh_key = new_ref[...].astype(F32)
    new_score = jnp.sum(own.astype(F32) * fresh_key, axis=1, keepdims=True) * SCALE
    state = (new_score, jnp.ones((H, 1), F32), jnp.broadcast_to(fresh_key[:, :LAT], (H, LAT)))
    length = length_ref[0, lax.axis_index("batch")] * BLOCK
    loads[2].wait()

    def suffix_step(c, state):
        start = pl.multiple_of(c * CHUNK, CHUNK)
        token = lax.broadcasted_iota(jnp.int32, (1, CHUNK), 1) + start
        bias = jnp.where(token < length, 0.0, -jnp.inf).astype(F32)
        return attend_chunk(state, own, suffix[pl.ds(start, CHUNK), :], bias)

    own_state = lax.fori_loop(0, suffix.shape[0] // CHUNK, suffix_step, state)
    loads[3].wait()

    rows = GROUP * H
    p_copies = []
    lane = lax.broadcasted_iota(jnp.int32, (rows, 128), 1)
    for g in range(n // GROUP):
        for j in range(GROUP):
            if g * GROUP + j > 0:
                q_copies[g * GROUP + j - 1].wait_recv()
        if g == 0:
            fill = rows - H
            start_state = (
                jnp.concatenate([own_state[0], jnp.full((fill, 1), FLOOR, F32)], axis=0),
                jnp.concatenate([own_state[1], jnp.zeros((fill, 1), F32)], axis=0),
                jnp.concatenate([own_state[2], jnp.zeros((fill, LAT), F32)], axis=0),
            )
        else:
            start_state = (jnp.full((rows, 1), FLOOR, F32), jnp.zeros((rows, 1), F32), jnp.zeros((rows, LAT), F32))
        group_queries = queries[g * GROUP : (g + 1) * GROUP].reshape(rows, KV)

        def prefix_step(c, state, g=g, group_queries=group_queries):
            start = pl.multiple_of(c * CHUNK, CHUNK)
            bias = jnp.concatenate(
                [jnp.broadcast_to(bias_scr[pl.ds(peers[g * GROUP + j], 1), pl.ds(start, CHUNK)], (H, CHUNK))
                 for j in range(GROUP)], axis=0)
            return attend_chunk(state, group_queries, prefix[pl.ds(start, CHUNK), :], bias)

        peak, total, sums = lax.fori_loop(0, prefix.shape[0] // CHUNK, prefix_step, start_state)
        stats = jnp.zeros((rows, 128), F32)
        for i, piece in enumerate(split3(peak) + split3(total)):
            stats = jnp.where(lane == i, piece, stats)
        span = slice(g * GROUP * heads_here, (g + 1) * GROUP * heads_here)
        for d in range(n):
            pick = [slice(j * H + d * heads_here, j * H + (d + 1) * heads_here) for j in range(GROUP)]
            send[d, span, :LAT] = jnp.concatenate([sums[s] for s in pick], axis=0).astype(BF16)
            send[d, span, LAT:] = jnp.concatenate([stats[s] for s in pick], axis=0).astype(BF16)
        for k in range(1, n):
            copy = pltpu.make_async_remote_copy(
                src_ref=send.at[peers[k], span], dst_ref=recv.at[k, span],
                send_sem=p_send.at[g, k], recv_sem=p_recv.at[g, k],
                device_id={"blk": peers[k]}, device_id_type=pl.DeviceIdType.MESH)
            copy.start()
            p_copies.append(copy)

    recv[0] = send[me]
    for copy in p_copies:
        copy.wait_recv()

    for q in range(n):
        parts = []
        for k in range(n):
            j = k ^ q
            block = recv[k, j * heads_here : (j + 1) * heads_here, :].astype(F32)
            stats = block[:, LAT:]
            m = stats[:, 0:1] + stats[:, 1:2] + stats[:, 2:3]
            l = stats[:, 3:4] + stats[:, 4:5] + stats[:, 5:6]
            parts.append((m, l, block[:, :LAT]))
        peak = functools.reduce(jnp.maximum, [p[0] for p in parts])
        total = jnp.zeros_like(peak)
        sums = jnp.zeros((heads_here, LAT), F32)
        for m, l, s in parts:
            w = jnp.exp2(m - peak)
            total = total + w * l
            sums = sums + w * s
        context = sums / total
        for lt in range(LAT // 128):
            ctx_scr[lt, q * heads_here : (q + 1) * heads_here, :] = context[:, lt * 128 : (lt + 1) * 128]

    for i in (4, 5, 6, 7):
        loads[i].wait()
    outs = []
    for h in range(heads_here):
        rows_h = jnp.concatenate(
            [ctx_scr[lt, pl.ds(h, n, stride=heads_here), :] for lt in range(LAT // 128)], axis=1)
        outs.append(jnp.dot(rows_h.astype(BF16), up[h], preferred_element_type=F32))
    head_out = jnp.concatenate(outs, axis=1).astype(BF16)
    request = lax.broadcasted_iota(jnp.int32, (n, RANK), 0)
    tenant_of = jnp.zeros((n, RANK), jnp.int32)
    for q in range(n):
        tenant_of = jnp.where(request == q, tenant_ref[peers[q]], tenant_of)
    lows = []
    for t in range(tenants):
        low = jnp.dot(head_out, oa[t], preferred_element_type=F32)
        lows.append(jnp.where(tenant_of == t, low, 0.0))
    low_out = jnp.concatenate(split3(jnp.concatenate(lows, axis=1)), axis=0).astype(BF16)
    adapter_up = ob[...].reshape(tenants * RANK, D)
    width = D // PARTS
    for c in range(PARTS // 2):
        columns = slice(c * 2 * width, (c + 1) * 2 * width)
        projected = jnp.dot(head_out, weight[:, columns], preferred_element_type=F32)
        added = jnp.dot(low_out, adapter_up[:, columns], preferred_element_type=F32)
        projected = projected + (added[:n] + added[n : 2 * n] + added[2 * n :])
        for half in range(2):
            for lt in range(width // 128):
                row_scr[lt, (2 * c + half) * n : (2 * c + half + 1) * n, :] = projected[
                    :, half * width + lt * 128 : half * width + (lt + 1) * 128]
    o_copies = []
    for q in list(range(1, n)) + [0]:
        target = out_recv if q == 0 else out_send
        for lt in range(width // 128):
            target[q, :, lt * 128 : (lt + 1) * 128] = row_scr[lt, pl.ds(q, PARTS, stride=n), :].astype(BF16)
        if q:
            copy = pltpu.make_async_remote_copy(
                src_ref=out_send.at[q], dst_ref=out_recv.at[q], send_sem=o_send.at[q], recv_sem=o_recv.at[q],
                device_id={"blk": peers[q]}, device_id_type=pl.DeviceIdType.MESH)
            copy.start()
            o_copies.append(copy)
    result = out_recv[0].astype(F32)
    for q in range(1, n):
        o_copies[q - 1].wait_recv()
        result = result + out_recv[q].astype(F32)
    out_ref[...] = result.astype(BF16)
    for copy in q_copies + p_copies + o_copies:
        copy.wait_send()


def on_device(
    query_base, query_latent, tenant_ids, adapter_qa, adapter_qb, prefix_cache, prefix_mask, suffix_cache,
    suffix_blocks, new_latent, value_up, out_weight, adapter_oa, adapter_ob,
):
    n = lax.axis_size("blk")
    vmem = pl.BlockSpec(memory_space=pltpu.VMEM)
    smem = pl.BlockSpec(memory_space=pltpu.SMEM)
    hbm = pl.BlockSpec(memory_space=pl.ANY)
    dma = pltpu.SemaphoreType.DMA
    slots = prefix_cache.shape[0]
    heads_here = H // n
    out = pl.pallas_call(
        functools.partial(kernel, n),
        out_shape=jax.ShapeDtypeStruct((PARTS, D // PARTS), BF16),
        in_specs=[smem, smem, vmem, vmem, hbm, hbm, hbm, vmem, hbm, vmem, hbm, hbm, hbm, hbm],
        out_specs=vmem,
        scratch_shapes=[
            pltpu.VMEM(adapter_qa.shape, BF16),
            pltpu.VMEM(adapter_qb.shape, BF16),
            pltpu.VMEM(prefix_cache.shape, BF16),
            pltpu.VMEM(suffix_cache.shape[1:], BF16),
            pltpu.VMEM(value_up.shape, BF16),
            pltpu.VMEM(out_weight.shape, BF16),
            pltpu.VMEM(adapter_oa.shape, BF16),
            pltpu.VMEM(adapter_ob.shape, BF16),
            pltpu.VMEM((H // 2, 2 * KV), F32),
            pltpu.VMEM((pl.cdiv(KV, 128), H, 128), F32),
            pltpu.VMEM((n, H, KV), BF16),
            pltpu.VMEM((n, slots), F32),
            pltpu.VMEM((8, 128), F32),
            pltpu.VMEM((8, 128), F32),
            pltpu.VMEM((n, n * heads_here, LAT + 128), BF16),
            pltpu.VMEM((n, n * heads_here, LAT + 128), BF16),
            pltpu.VMEM((LAT // 128, n * heads_here, 128), F32),
            pltpu.VMEM((D // PARTS // 128, PARTS * n, 128), F32),
            pltpu.VMEM((n, PARTS, D // PARTS), BF16),
            pltpu.VMEM((n, PARTS, D // PARTS), BF16),
            dma((8,)), dma((n,)), dma((n,)), dma((n // GROUP, n)), dma((n // GROUP, n)), dma((n,)), dma((n,)),
        ],
        compiler_params=pltpu.CompilerParams(
            collective_id=0, has_side_effects=True, vmem_limit_bytes=60 << 20),
    )(
        tenant_ids, suffix_blocks, query_base, query_latent, adapter_qa, adapter_qb, prefix_cache, prefix_mask,
        suffix_cache, new_latent, value_up, out_weight, adapter_oa, adapter_ob,
    )
    return out.reshape(1, D)


def solution(mesh):
    placed = (
        P(("batch", "blk"), None),
        P(("batch", "blk"), None),
        P("batch"),
        P(),
        P(),
        P("blk", None),
        P("batch", "blk"),
        P(("batch", "blk"), None, None),
        P("blk", None),
        P(("batch", "blk"), None),
        P("blk", None, None),
        P("blk", None),
        P(None, "blk", None),
        P(),
    )
    return jax.shard_map(
        on_device, mesh=mesh, in_specs=placed, out_specs=P(("batch", "blk"), None), check_vma=False
    )
```

```python
import functools
import math

import jax
import jax.numpy as jnp
from jax import lax
from jax.experimental import pallas as pl
from jax.experimental.pallas import tpu as pltpu
from jax.sharding import PartitionSpec as P

D = 7168
H = 64
LAT = 512
QK = 192
RANK = 16
BLOCK = 128
KV = 576
FLOOR = -1e30
CHUNK = 1024
GROUP = 4
PARTS = 8
SCALE = QK ** (-0.5) * math.log2(math.e)
F32 = jnp.float32
BF16 = jnp.bfloat16
NT = (((1,), (1,)), ((), ()))


def split3(x):
    hi = x.astype(BF16).astype(F32)
    rest = x - hi
    mid = rest.astype(BF16).astype(F32)
    return hi, mid, rest - mid


def attend_chunk(state, queries, keys, bias):
    peak, total, sums = state
    scores = jnp.dot(queries, keys, preferred_element_type=F32) * SCALE + bias
    fresh = jnp.maximum(peak, jnp.max(scores, axis=1, keepdims=True))
    weights = jnp.exp2(scores - fresh)
    keep = jnp.exp2(peak - fresh)
    total = total * keep + jnp.sum(weights, axis=1, keepdims=True)
    sums = sums * keep + lax.dot_general(
        weights.astype(BF16), keys[:LAT], NT, preferred_element_type=F32)
    return fresh, total, sums


def kernel(
    n,
    tenant_ref, length_ref,
    base_ref, latent_ref, qa_hbm, qb_hbm, prefix_hbm, mask_ref, suffix_hbm, new_ref,
    up_hbm, weight_hbm, oa_hbm, ob_hbm,
    out_ref,
    qa, qb, prefix, suffix, up, weight, oa, ob,
    pair_scr, head_scr, queries, bias_scr, send, recv, ctx_scr, row_scr, out_send, out_recv,
    load_sem, q_send, q_recv, p_send, p_recv, o_send, o_recv,
):
    me = lax.axis_index("blk")
    bits = n.bit_length() - 1
    heads_here = H // n

    def peer(k):
        total = 0
        for b in range(bits):
            total = total + lax.rem(lax.div(me, 1 << b) + (k >> b & 1), 2) * (1 << b)
        return total

    peers = [peer(k) for k in range(n)]
    loads = [
        pltpu.make_async_copy(src, dst, load_sem.at[i])
        for i, (src, dst) in enumerate(
            [(qa_hbm, qa), (qb_hbm, qb), (suffix_hbm.at[0], suffix), (prefix_hbm, prefix),
             (up_hbm, up), (oa_hbm, oa), (ob_hbm, ob), (weight_hbm, weight)]
        )
    ]
    for load in loads:
        load.start()

    barrier = pltpu.get_barrier_semaphore()
    for k in range(1, n):
        pl.semaphore_signal(barrier, inc=1, device_id={"blk": peers[k]}, device_id_type=pl.DeviceIdType.MESH)

    loads[0].wait()
    own_tenant = tenant_ref[me]
    latent = jnp.broadcast_to(latent_ref[...].astype(F32), (16, latent_ref.shape[1])).astype(BF16)
    tenants = qa.shape[0]
    lows = []
    for t in range(tenants):
        low = lax.dot_general(latent, qa[t], NT, preferred_element_type=F32)
        lows.append(jnp.where(own_tenant == t, low, 0.0))
    low_spread = jnp.concatenate(lows, axis=1).astype(BF16)
    loads[1].wait()
    row_id = lax.broadcasted_iota(jnp.int32, (8, 2 * KV), 0)
    for i in range(H // 16):
        columns = slice(i * 16 * KV, (i + 1) * 16 * KV)
        up_map = qb[:, :, columns].reshape(tenants * RANK, 16 * KV)
        delta = jnp.dot(low_spread, up_map, preferred_element_type=F32)[:8]
        full = delta + base_ref[:, columns].astype(F32)
        rows = full[:, : 2 * KV]
        for p in range(1, 8):
            rows = jnp.where(row_id == p, full[:, p * 2 * KV : (p + 1) * 2 * KV], rows)
        pair_scr[i * 8 : (i + 1) * 8, :] = rows
    even = pair_scr[:, :KV]
    odd = pair_scr[:, KV:]
    tiles = [(lt, min(128, KV - lt * 128)) for lt in range(pl.cdiv(KV, 128))]
    for lt, width in tiles:
        head_scr[lt, pl.ds(0, H // 2, stride=2), :width] = even[:, lt * 128 : lt * 128 + width]
        head_scr[lt, pl.ds(1, H // 2, stride=2), :width] = odd[:, lt * 128 : lt * 128 + width]
    for lt, width in tiles:
        queries[0, :, lt * 128 : lt * 128 + width] = head_scr[lt, :, :width].astype(BF16)

    pl.semaphore_wait(barrier, n - 1)
    q_copies = []
    for k in range(1, n):
        copy = pltpu.make_async_remote_copy(
            src_ref=queries.at[0], dst_ref=queries.at[k], send_sem=q_send.at[k], recv_sem=q_recv.at[k],
            device_id={"blk": peers[k]}, device_id_type=pl.DeviceIdType.MESH)
        copy.start()
        q_copies.append(copy)

    live = jnp.where(mask_ref[...] > 0, 0.0, -jnp.inf).astype(F32)
    for b in range(mask_ref.shape[1]):
        bias_scr[:, b * BLOCK : (b + 1) * BLOCK] = jnp.broadcast_to(live[:, b : b + 1], (n, BLOCK))

    own = queries[0]
    fresh_key = new_ref[...].astype(F32)
    new_score = jnp.sum(own.astype(F32) * fresh_key, axis=1, keepdims=True) * SCALE
    state = (new_score, jnp.ones((H, 1), F32), jnp.broadcast_to(fresh_key[:, :LAT], (H, LAT)))
    length = length_ref[0, lax.axis_index("batch")] * BLOCK
    loads[2].wait()

    def suffix_step(c, state):
        start = pl.multiple_of(c * CHUNK, CHUNK)
        token = lax.broadcasted_iota(jnp.int32, (1, CHUNK), 1) + start
        bias = jnp.where(token < length, 0.0, -jnp.inf).astype(F32)
        return attend_chunk(state, own, suffix[:, pl.ds(start, CHUNK)], bias)

    own_state = lax.fori_loop(0, suffix.shape[1] // CHUNK, suffix_step, state)
    loads[3].wait()

    rows = GROUP * H
    p_copies = []
    lane = lax.broadcasted_iota(jnp.int32, (rows, 128), 1)
    for g in range(n // GROUP):
        for j in range(GROUP):
            if g * GROUP + j > 0:
                q_copies[g * GROUP + j - 1].wait_recv()
        if g == 0:
            fill = rows - H
            start_state = (
                jnp.concatenate([own_state[0], jnp.full((fill, 1), FLOOR, F32)], axis=0),
                jnp.concatenate([own_state[1], jnp.zeros((fill, 1), F32)], axis=0),
                jnp.concatenate([own_state[2], jnp.zeros((fill, LAT), F32)], axis=0),
            )
        else:
            start_state = (jnp.full((rows, 1), FLOOR, F32), jnp.zeros((rows, 1), F32), jnp.zeros((rows, LAT), F32))
        group_queries = queries[g * GROUP : (g + 1) * GROUP].reshape(rows, KV)

        def prefix_step(c, state, g=g, group_queries=group_queries):
            start = pl.multiple_of(c * CHUNK, CHUNK)
            bias = jnp.concatenate(
                [jnp.broadcast_to(bias_scr[pl.ds(peers[g * GROUP + j], 1), pl.ds(start, CHUNK)], (H, CHUNK))
                 for j in range(GROUP)], axis=0)
            return attend_chunk(state, group_queries, prefix[:, pl.ds(start, CHUNK)], bias)

        peak, total, sums = lax.fori_loop(0, prefix.shape[1] // CHUNK, prefix_step, start_state)
        stats = jnp.zeros((rows, 128), F32)
        for i, piece in enumerate(split3(peak) + split3(total)):
            stats = jnp.where(lane == i, piece, stats)
        span = slice(g * GROUP * heads_here, (g + 1) * GROUP * heads_here)
        for d in range(n):
            pick = [slice(j * H + d * heads_here, j * H + (d + 1) * heads_here) for j in range(GROUP)]
            send[d, span, :LAT] = jnp.concatenate([sums[s] for s in pick], axis=0).astype(BF16)
            send[d, span, LAT:] = jnp.concatenate([stats[s] for s in pick], axis=0).astype(BF16)
        for k in range(1, n):
            copy = pltpu.make_async_remote_copy(
                src_ref=send.at[peers[k], span], dst_ref=recv.at[k, span],
                send_sem=p_send.at[g, k], recv_sem=p_recv.at[g, k],
                device_id={"blk": peers[k]}, device_id_type=pl.DeviceIdType.MESH)
            copy.start()
            p_copies.append(copy)

    recv[0] = send[me]
    for copy in p_copies:
        copy.wait_recv()

    for q in range(n):
        parts = []
        for k in range(n):
            j = k ^ q
            block = recv[k, j * heads_here : (j + 1) * heads_here, :].astype(F32)
            stats = block[:, LAT:]
            m = stats[:, 0:1] + stats[:, 1:2] + stats[:, 2:3]
            l = stats[:, 3:4] + stats[:, 4:5] + stats[:, 5:6]
            parts.append((m, l, block[:, :LAT]))
        peak = functools.reduce(jnp.maximum, [p[0] for p in parts])
        total = jnp.zeros_like(peak)
        sums = jnp.zeros((heads_here, LAT), F32)
        for m, l, s in parts:
            w = jnp.exp2(m - peak)
            total = total + w * l
            sums = sums + w * s
        context = sums / total
        for lt in range(LAT // 128):
            ctx_scr[lt, q * heads_here : (q + 1) * heads_here, :] = context[:, lt * 128 : (lt + 1) * 128]

    for i in (4, 5, 6, 7):
        loads[i].wait()
    outs = []
    for h in range(heads_here):
        rows_h = jnp.concatenate(
            [ctx_scr[lt, pl.ds(h, n, stride=heads_here), :] for lt in range(LAT // 128)], axis=1)
        outs.append(jnp.dot(rows_h.astype(BF16), up[h], preferred_element_type=F32))
    head_out = jnp.concatenate(outs, axis=1).astype(BF16)
    request = lax.broadcasted_iota(jnp.int32, (n, RANK), 0)
    tenant_of = jnp.zeros((n, RANK), jnp.int32)
    for q in range(n):
        tenant_of = jnp.where(request == q, tenant_ref[peers[q]], tenant_of)
    lows = []
    for t in range(tenants):
        low = lax.dot_general(head_out, oa[t], NT, preferred_element_type=F32)
        lows.append(jnp.where(tenant_of == t, low, 0.0))
    low_out = jnp.concatenate(split3(jnp.concatenate(lows, axis=1)), axis=0).astype(BF16)
    adapter_up = ob[...].reshape(tenants * RANK, D)
    width = D // PARTS
    for c in range(PARTS // 2):
        columns = slice(c * 2 * width, (c + 1) * 2 * width)
        projected = jnp.dot(head_out, weight[:, columns], preferred_element_type=F32)
        added = jnp.dot(low_out, adapter_up[:, columns], preferred_element_type=F32)
        projected = projected + (added[:n] + added[n : 2 * n] + added[2 * n :])
        for half in range(2):
            for lt in range(width // 128):
                row_scr[lt, (2 * c + half) * n : (2 * c + half + 1) * n, :] = projected[
                    :, half * width + lt * 128 : half * width + (lt + 1) * 128]
    o_copies = []
    for q in list(range(1, n)) + [0]:
        target = out_recv if q == 0 else out_send
        for lt in range(width // 128):
            target[q, :, lt * 128 : (lt + 1) * 128] = row_scr[lt, pl.ds(q, PARTS, stride=n), :].astype(BF16)
        if q:
            copy = pltpu.make_async_remote_copy(
                src_ref=out_send.at[q], dst_ref=out_recv.at[q], send_sem=o_send.at[q], recv_sem=o_recv.at[q],
                device_id={"blk": peers[q]}, device_id_type=pl.DeviceIdType.MESH)
            copy.start()
            o_copies.append(copy)
    result = out_recv[0].astype(F32)
    for q in range(1, n):
        o_copies[q - 1].wait_recv()
        result = result + out_recv[q].astype(F32)
    out_ref[...] = result.astype(BF16)
    for copy in q_copies + p_copies + o_copies:
        copy.wait_send()


def on_device(
    query_base, query_latent, tenant_ids, adapter_qa, adapter_qb, prefix_cache, prefix_mask, suffix_cache,
    suffix_blocks, new_latent, value_up, out_weight, adapter_oa, adapter_ob,
):
    n = lax.axis_size("blk")
    prefix_cache = prefix_cache.T
    suffix_cache = suffix_cache.transpose(0, 2, 1)
    adapter_qa = adapter_qa.transpose(0, 2, 1)
    adapter_oa = adapter_oa.transpose(0, 2, 1)
    vmem = pl.BlockSpec(memory_space=pltpu.VMEM)
    smem = pl.BlockSpec(memory_space=pltpu.SMEM)
    hbm = pl.BlockSpec(memory_space=pl.ANY)
    dma = pltpu.SemaphoreType.DMA
    slots = prefix_cache.shape[1]
    heads_here = H // n
    out = pl.pallas_call(
        functools.partial(kernel, n),
        out_shape=jax.ShapeDtypeStruct((PARTS, D // PARTS), BF16),
        in_specs=[smem, smem, vmem, vmem, hbm, hbm, hbm, vmem, hbm, vmem, hbm, hbm, hbm, hbm],
        out_specs=vmem,
        scratch_shapes=[
            pltpu.VMEM(adapter_qa.shape, BF16),
            pltpu.VMEM(adapter_qb.shape, BF16),
            pltpu.VMEM(prefix_cache.shape, BF16),
            pltpu.VMEM(suffix_cache.shape[1:], BF16),
            pltpu.VMEM(value_up.shape, BF16),
            pltpu.VMEM(out_weight.shape, BF16),
            pltpu.VMEM(adapter_oa.shape, BF16),
            pltpu.VMEM(adapter_ob.shape, BF16),
            pltpu.VMEM((H // 2, 2 * KV), F32),
            pltpu.VMEM((pl.cdiv(KV, 128), H, 128), F32),
            pltpu.VMEM((n, H, KV), BF16),
            pltpu.VMEM((n, slots), F32),
            pltpu.VMEM((n, n * heads_here, LAT + 128), BF16),
            pltpu.VMEM((n, n * heads_here, LAT + 128), BF16),
            pltpu.VMEM((LAT // 128, n * heads_here, 128), F32),
            pltpu.VMEM((D // PARTS // 128, PARTS * n, 128), F32),
            pltpu.VMEM((n, PARTS, D // PARTS), BF16),
            pltpu.VMEM((n, PARTS, D // PARTS), BF16),
            dma((8,)), dma((n,)), dma((n,)), dma((n // GROUP, n)), dma((n // GROUP, n)), dma((n,)), dma((n,)),
        ],
        compiler_params=pltpu.CompilerParams(
            collective_id=0, has_side_effects=True, vmem_limit_bytes=60 << 20),
    )(
        tenant_ids, suffix_blocks, query_base, query_latent, adapter_qa, adapter_qb, prefix_cache, prefix_mask,
        suffix_cache, new_latent, value_up, out_weight, adapter_oa, adapter_ob,
    )
    return out.reshape(1, D)


def solution(mesh):
    placed = (
        P(("batch", "blk"), None),
        P(("batch", "blk"), None),
        P("batch"),
        P(),
        P(),
        P("blk", None),
        P("batch", "blk"),
        P(("batch", "blk"), None, None),
        P("blk", None),
        P(("batch", "blk"), None),
        P("blk", None, None),
        P("blk", None),
        P(None, "blk", None),
        P(),
    )
    return jax.shard_map(
        on_device, mesh=mesh, in_specs=placed, out_specs=P(("batch", "blk"), None), check_vma=False
    )
```

```python
import functools
import math

import jax
import jax.numpy as jnp
from jax import lax
from jax.experimental import pallas as pl
from jax.experimental.pallas import tpu as pltpu
from jax.sharding import PartitionSpec as P

D = 7168
H = 64
LAT = 512
QK = 192
RANK = 16
BLOCK = 128
KV = 576
FLOOR = -1e30
CHUNK = 2048
GROUP = 4
PARTS = 8
SCALE = QK ** (-0.5) * math.log2(math.e)
F32 = jnp.float32
BF16 = jnp.bfloat16
NT = (((1,), (1,)), ((), ()))


def split3(x):
    hi = x.astype(BF16).astype(F32)
    rest = x - hi
    mid = rest.astype(BF16).astype(F32)
    return hi, mid, rest - mid


def attend_chunk(state, queries, keys, bias):
    peak, total, sums = state
    scores = jnp.dot(queries, keys, preferred_element_type=F32) * SCALE + bias
    fresh = jnp.maximum(peak, jnp.max(scores, axis=1, keepdims=True))
    weights = jnp.exp2(scores - fresh)
    keep = jnp.exp2(peak - fresh)
    total = total * keep + jnp.sum(weights, axis=1, keepdims=True)
    sums = sums * keep + lax.dot_general(
        weights.astype(BF16), keys[:LAT], NT, preferred_element_type=F32)
    return fresh, total, sums


def kernel(
    n,
    tenant_ref, length_ref,
    base_ref, latent_ref, qa_hbm, qb_hbm, prefix_hbm, mask_ref, suffix_hbm, new_ref,
    up_hbm, weight_hbm, oa_hbm, ob_hbm,
    out_ref,
    qa, qb, prefix, suffix, up, weight, oa, ob,
    pair_scr, head_scr, queries, bias_scr, send, recv, ctx_scr, row_scr, out_send, out_recv,
    early_sem, load_sem, q_send, q_recv, p_send, p_recv, o_send, o_recv,
):
    me = lax.axis_index("blk")
    bits = n.bit_length() - 1
    heads_here = H // n

    def peer(k):
        total = 0
        for b in range(bits):
            total = total + lax.rem(lax.div(me, 1 << b) + (k >> b & 1), 2) * (1 << b)
        return total

    peers = [peer(k) for k in range(n)]
    span_q = qb.shape[2] // 4
    early = [pltpu.make_async_copy(qa_hbm, qa, early_sem.at[4])] + [
        pltpu.make_async_copy(
            qb_hbm.at[:, :, i * span_q : (i + 1) * span_q], qb.at[:, :, i * span_q : (i + 1) * span_q], early_sem.at[i])
        for i in range(4)
    ]
    loads = [
        pltpu.make_async_copy(src, dst, load_sem.at[i])
        for i, (src, dst) in enumerate(
            [(suffix_hbm.at[0], suffix), (prefix_hbm, prefix),
             (up_hbm, up), (oa_hbm, oa), (ob_hbm, ob), (weight_hbm, weight)]
        )
    ]
    for load in early:
        load.start()

    barrier = pltpu.get_barrier_semaphore()
    for k in range(1, n):
        pl.semaphore_signal(barrier, inc=1, device_id={"blk": peers[k]}, device_id_type=pl.DeviceIdType.MESH)

    early[0].wait()
    own_tenant = tenant_ref[me]
    latent = jnp.broadcast_to(latent_ref[...].astype(F32), (16, latent_ref.shape[1])).astype(BF16)
    tenants = qa.shape[0]
    lane_tenant = lax.broadcasted_iota(jnp.int32, (16, tenants * RANK), 1) // RANK
    low = lax.dot_general(latent, qa[...].reshape(tenants * RANK, qa.shape[2]), NT, preferred_element_type=F32)
    low_spread = jnp.where(lane_tenant == own_tenant, low, 0.0).astype(BF16)
    row_id = lax.broadcasted_iota(jnp.int32, (8, 2 * KV), 0)
    for i in range(H // 16):
        columns = slice(i * 16 * KV, (i + 1) * 16 * KV)
        early[i + 1].wait()
        if i >= 2:
            loads[i - 2].start()
        up_map = qb[:, :, columns].reshape(tenants * RANK, 16 * KV)
        delta = jnp.dot(low_spread, up_map, preferred_element_type=F32)[:8]
        full = delta + base_ref[:, columns].astype(F32)
        rows = full[:, : 2 * KV]
        for p in range(1, 8):
            rows = jnp.where(row_id == p, full[:, p * 2 * KV : (p + 1) * 2 * KV], rows)
        pair_scr[i * 8 : (i + 1) * 8, :] = rows
    even = pair_scr[:, :KV]
    odd = pair_scr[:, KV:]
    tiles = [(lt, min(128, KV - lt * 128)) for lt in range(pl.cdiv(KV, 128))]
    for lt, width in tiles:
        head_scr[lt, pl.ds(0, H // 2, stride=2), :width] = even[:, lt * 128 : lt * 128 + width]
        head_scr[lt, pl.ds(1, H // 2, stride=2), :width] = odd[:, lt * 128 : lt * 128 + width]
    for lt, width in tiles:
        queries[0, :, lt * 128 : lt * 128 + width] = head_scr[lt, :, :width].astype(BF16)

    pl.semaphore_wait(barrier, n - 1)
    order = [0, 1] + list(range(2, n, 2)) + list(range(3, n, 2))
    place = [order.index(k) for k in range(n)]
    q_copies = {}

    def send_query(source, target, to):
        copy = pltpu.make_async_remote_copy(
            src_ref=queries.at[place[source]], dst_ref=queries.at[place[target]],
            send_sem=q_send.at[target], recv_sem=q_recv.at[target],
            device_id={"blk": peers[to]}, device_id_type=pl.DeviceIdType.MESH)
        copy.start()
        q_copies[target] = copy

    def forward(k):
        q_copies[k].wait_recv()
        send_query(k, k + 1, 1)

    for k in list(range(2, n, 2)) + [1]:
        send_query(0, k, k)
    for load in loads[2:]:
        load.start()

    live = jnp.where(mask_ref[...] > 0, 0.0, -jnp.inf).astype(F32)
    for b in range(mask_ref.shape[1]):
        bias_scr[:, b * BLOCK : (b + 1) * BLOCK] = jnp.broadcast_to(live[:, b : b + 1], (n, BLOCK))

    own = queries[0]
    fresh_key = new_ref[...].astype(F32)
    new_score = jnp.sum(own.astype(F32) * fresh_key, axis=1, keepdims=True) * SCALE
    state = (new_score, jnp.ones((H, 1), F32), jnp.broadcast_to(fresh_key[:, :LAT], (H, LAT)))
    length = length_ref[0, lax.axis_index("batch")] * BLOCK
    loads[0].wait()

    def suffix_step(c, state):
        start = pl.multiple_of(c * CHUNK, CHUNK)
        token = lax.broadcasted_iota(jnp.int32, (1, CHUNK), 1) + start
        bias = jnp.where(token < length, 0.0, -jnp.inf).astype(F32)
        return attend_chunk(state, own, suffix[:, pl.ds(start, CHUNK)], bias)

    own_state = lax.fori_loop(0, suffix.shape[1] // CHUNK, suffix_step, state, unroll=True)
    loads[1].wait()

    rows = GROUP * H
    p_copies = []
    lane = lax.broadcasted_iota(jnp.int32, (rows, 128), 1)
    for g in range(n // GROUP):
        members = order[g * GROUP : (g + 1) * GROUP]
        for j in members:
            if g == 0 and j >= 2:
                forward(j)
            elif j % 2:
                q_copies[j].wait_recv()
        if g == 0:
            fill = rows - H
            start_state = (
                jnp.concatenate([own_state[0], jnp.full((fill, 1), FLOOR, F32)], axis=0),
                jnp.concatenate([own_state[1], jnp.zeros((fill, 1), F32)], axis=0),
                jnp.concatenate([own_state[2], jnp.zeros((fill, LAT), F32)], axis=0),
            )
        else:
            start_state = (jnp.full((rows, 1), FLOOR, F32), jnp.zeros((rows, 1), F32), jnp.zeros((rows, LAT), F32))
        group_queries = queries[g * GROUP : (g + 1) * GROUP].reshape(rows, KV)

        def prefix_step(c, state, members=members, group_queries=group_queries):
            start = pl.multiple_of(c * CHUNK, CHUNK)
            bias = jnp.concatenate(
                [jnp.broadcast_to(bias_scr[pl.ds(peers[j], 1), pl.ds(start, CHUNK)], (H, CHUNK))
                 for j in members], axis=0)
            return attend_chunk(state, group_queries, prefix[:, pl.ds(start, CHUNK)], bias)

        chunks = prefix.shape[1] // CHUNK
        middle = 0
        if g == 0:
            middle = chunks // 2
            start_state = lax.fori_loop(0, middle, prefix_step, start_state, unroll=True)
            for j in order[GROUP:]:
                if j % 2 == 0:
                    forward(j)
        peak, total, sums = lax.fori_loop(middle, chunks, prefix_step, start_state, unroll=True)
        stats = jnp.zeros((rows, 128), F32)
        for i, piece in enumerate(split3(peak) + split3(total)):
            stats = jnp.where(lane == i, piece, stats)
        span = slice(g * GROUP * heads_here, (g + 1) * GROUP * heads_here)
        for d in range(n):
            pick = [slice(j * H + d * heads_here, j * H + (d + 1) * heads_here) for j in range(GROUP)]
            send[d, span, :LAT] = jnp.concatenate([sums[s] for s in pick], axis=0).astype(BF16)
            send[d, span, LAT:] = jnp.concatenate([stats[s] for s in pick], axis=0).astype(BF16)
        for k in [k for k in order[::-1] if k > 1] + [1]:
            copy = pltpu.make_async_remote_copy(
                src_ref=send.at[peers[k], span], dst_ref=recv.at[k, span],
                send_sem=p_send.at[g, k], recv_sem=p_recv.at[g, k],
                device_id={"blk": peers[k]}, device_id_type=pl.DeviceIdType.MESH)
            copy.start()
            p_copies.append(copy)

    recv[0] = send[me]
    for copy in p_copies:
        copy.wait_recv()

    for q in range(n):
        parts = []
        for k in range(n):
            j = place[k ^ q]
            block = recv[k, j * heads_here : (j + 1) * heads_here, :].astype(F32)
            stats = block[:, LAT:]
            m = stats[:, 0:1] + stats[:, 1:2] + stats[:, 2:3]
            l = stats[:, 3:4] + stats[:, 4:5] + stats[:, 5:6]
            parts.append((m, l, block[:, :LAT]))
        peak = functools.reduce(jnp.maximum, [p[0] for p in parts])
        total = jnp.zeros_like(peak)
        sums = jnp.zeros((heads_here, LAT), F32)
        for m, l, s in parts:
            w = jnp.exp2(m - peak)
            total = total + w * l
            sums = sums + w * s
        context = sums / total
        for lt in range(LAT // 128):
            ctx_scr[lt, q * heads_here : (q + 1) * heads_here, :] = context[:, lt * 128 : (lt + 1) * 128]

    for i in (2, 3, 4, 5):
        loads[i].wait()
    outs = []
    for h in range(heads_here):
        rows_h = jnp.concatenate(
            [ctx_scr[lt, pl.ds(h, n, stride=heads_here), :] for lt in range(LAT // 128)], axis=1)
        outs.append(jnp.dot(rows_h.astype(BF16), up[h], preferred_element_type=F32))
    head_out = jnp.concatenate(outs, axis=1).astype(BF16)
    request = lax.broadcasted_iota(jnp.int32, (n, tenants * RANK), 0)
    tenant_of = jnp.zeros((n, tenants * RANK), jnp.int32)
    for q in range(n):
        tenant_of = jnp.where(request == q, tenant_ref[peers[q]], tenant_of)
    column_tenant = lax.broadcasted_iota(jnp.int32, (n, tenants * RANK), 1) // RANK
    low = lax.dot_general(head_out, oa[...].reshape(tenants * RANK, oa.shape[2]), NT, preferred_element_type=F32)
    low = jnp.where(tenant_of == column_tenant, low, 0.0)
    low_out = jnp.concatenate(split3(low), axis=0).astype(BF16)
    adapter_up = ob[...].reshape(tenants * RANK, D)
    width = D // PARTS
    for c in range(PARTS // 2):
        columns = slice(c * 2 * width, (c + 1) * 2 * width)
        projected = jnp.dot(head_out, weight[:, columns], preferred_element_type=F32)
        added = jnp.dot(low_out, adapter_up[:, columns], preferred_element_type=F32)
        projected = projected + (added[:n] + added[n : 2 * n] + added[2 * n :])
        for half in range(2):
            for lt in range(width // 128):
                row_scr[lt, (2 * c + half) * n : (2 * c + half + 1) * n, :] = projected[
                    :, half * width + lt * 128 : half * width + (lt + 1) * 128]
    o_copies = []
    for q in list(range(1, n)) + [0]:
        target = out_recv if q == 0 else out_send
        for lt in range(width // 128):
            target[q, :, lt * 128 : (lt + 1) * 128] = row_scr[lt, pl.ds(q, PARTS, stride=n), :].astype(BF16)
        if q:
            copy = pltpu.make_async_remote_copy(
                src_ref=out_send.at[q], dst_ref=out_recv.at[q], send_sem=o_send.at[q], recv_sem=o_recv.at[q],
                device_id={"blk": peers[q]}, device_id_type=pl.DeviceIdType.MESH)
            copy.start()
            o_copies.append(copy)
    result = out_recv[0].astype(F32)
    for q in range(1, n):
        o_copies[q - 1].wait_recv()
        result = result + out_recv[q].astype(F32)
    out_ref[...] = result.astype(BF16)
    for copy in list(q_copies.values()) + p_copies + o_copies:
        copy.wait_send()


def on_device(
    query_base, query_latent, tenant_ids, adapter_qa, adapter_qb, prefix_cache, prefix_mask, suffix_cache,
    suffix_blocks, new_latent, value_up, out_weight, adapter_oa, adapter_ob,
):
    n = lax.axis_size("blk")
    prefix_cache = prefix_cache.T
    suffix_cache = suffix_cache.transpose(0, 2, 1)
    adapter_qa = adapter_qa.transpose(0, 2, 1)
    adapter_oa = adapter_oa.transpose(0, 2, 1)
    vmem = pl.BlockSpec(memory_space=pltpu.VMEM)
    smem = pl.BlockSpec(memory_space=pltpu.SMEM)
    hbm = pl.BlockSpec(memory_space=pl.ANY)
    dma = pltpu.SemaphoreType.DMA
    slots = prefix_cache.shape[1]
    heads_here = H // n
    out = pl.pallas_call(
        functools.partial(kernel, n),
        out_shape=jax.ShapeDtypeStruct((PARTS, D // PARTS), BF16),
        in_specs=[smem, smem, vmem, vmem, hbm, hbm, hbm, vmem, hbm, vmem, hbm, hbm, hbm, hbm],
        out_specs=vmem,
        scratch_shapes=[
            pltpu.VMEM(adapter_qa.shape, BF16),
            pltpu.VMEM(adapter_qb.shape, BF16),
            pltpu.VMEM(prefix_cache.shape, BF16),
            pltpu.VMEM(suffix_cache.shape[1:], BF16),
            pltpu.VMEM(value_up.shape, BF16),
            pltpu.VMEM(out_weight.shape, BF16),
            pltpu.VMEM(adapter_oa.shape, BF16),
            pltpu.VMEM(adapter_ob.shape, BF16),
            pltpu.VMEM((H // 2, 2 * KV), F32),
            pltpu.VMEM((pl.cdiv(KV, 128), H, 128), F32),
            pltpu.VMEM((n, H, KV), BF16),
            pltpu.VMEM((n, slots), F32),
            pltpu.VMEM((n, n * heads_here, LAT + 128), BF16),
            pltpu.VMEM((n, n * heads_here, LAT + 128), BF16),
            pltpu.VMEM((LAT // 128, n * heads_here, 128), F32),
            pltpu.VMEM((D // PARTS // 128, PARTS * n, 128), F32),
            pltpu.VMEM((n, PARTS, D // PARTS), BF16),
            pltpu.VMEM((n, PARTS, D // PARTS), BF16),
            dma((5,)), dma((6,)), dma((n,)), dma((n,)), dma((n // GROUP, n)), dma((n // GROUP, n)), dma((n,)), dma((n,)),
        ],
        compiler_params=pltpu.CompilerParams(
            collective_id=0, has_side_effects=True, vmem_limit_bytes=60 << 20),
    )(
        tenant_ids, suffix_blocks, query_base, query_latent, adapter_qa, adapter_qb, prefix_cache, prefix_mask,
        suffix_cache, new_latent, value_up, out_weight, adapter_oa, adapter_ob,
    )
    return out.reshape(1, D)


def solution(mesh):
    placed = (
        P(("batch", "blk"), None),
        P(("batch", "blk"), None),
        P("batch"),
        P(),
        P(),
        P("blk", None),
        P("batch", "blk"),
        P(("batch", "blk"), None, None),
        P("blk", None),
        P(("batch", "blk"), None),
        P("blk", None, None),
        P("blk", None),
        P(None, "blk", None),
        P(),
    )
    return jax.shard_map(
        on_device, mesh=mesh, in_specs=placed, out_specs=P(("batch", "blk"), None), check_vma=False
    )
```
